32 devices in a mesh: blk: 2 (over y), wide: 4 (over z), dp: 4 (over x, core).
Axes of the slice: x: 2, y: 2, z: 4, core: 2. Of those that a mesh axis runs over, the one named last changes fastest.
Arguments:
- token_ids: int32 [4096], P(('dp', 'blk', 'wide')), parts along dimension 0, may hold values from 0 to 5
- embedding: float32 [6, 1536], replicated, may hold values from -3 to 3
- queries: bfloat16 [4096, 768], P(('dp', 'blk', 'wide')), parts along dimension 0, may hold values from -12 to 12
- key_rows: bfloat16 [4096, 768], P(('dp', 'blk', 'wide')), parts along dimension 0, may hold values from -6 to 6
- value_rows: bfloat16 [4096, 768], P(('dp', 'blk', 'wide')), parts along dimension 0, may hold values from -6 to 6
- head_mixer: bfloat16 [768, 1536], replicated, may hold values from -0.21875 to 0.21875
- expand_weight: bfloat16 [1536, 3072], P(None, 'wide'), may hold values from -0.15625 to 0.15625
- reduce_weight: bfloat16 [3072, 1536], P('wide'), may hold values from -0.109375 to 0.109375
- cotangent: bfloat16 [4096, 1536], P(('dp', 'blk', 'wide')), parts along dimension 0, may hold values from -0.29882812 to 0.29882812
Outputs:
- restored: bfloat16 [4096, 1536], P(('dp', 'blk', 'wide')), parts along dimension 0
- expand_grad: float32 [6144, 3072], P(('dp', 'blk'), 'wide'), parts along dimension 0
- reduce_grad: float32 [12288, 1536], P(('dp', 'wide'), 'blk'), parts along dimension 0
The draws below stay inside these ranges and needn't reach their ends.
There are 4 independent parts, one for each index of `dp`. The reference program is written for one: setup_inputs(seed, part) draws one part's arguments, and reference() takes and returns one part's arrays. A program takes and returns all parts, laid end to end along the dimension named above; an argument that names none is the same for every part. Nothing has to cross between parts.
All inputs are finite; a program needn't handle non-finite values.
Results may differ from the reference program's by a relative error of at most 0.018.
Values may be sent and summed in bfloat16 or wider, within the bound.
No kernel may reach another device: no remote copies, remote signals or barrier semaphores. Data moves between devices by JAX's collectives and lax.ppermute only.
A program may use at most 128 MiB of HBM per device.

```python
import jax
import jax.numpy as jnp
from jax import lax

D = 1536
FINE_HEADS = 6
HEAD = 128
FF = 3072
VOCAB = 6
POOL = 8
QKV = 768
LENGTH = 1024


def draw_pair(key):
    array_shape = (LENGTH, QKV)
    query_base = jnp.clip(3.0 * jax.random.normal(jax.random.fold_in(key, 101), array_shape, jnp.float32), -12.0, 12.0)
    key_base = jnp.clip(jax.random.normal(jax.random.fold_in(key, 102), array_shape, jnp.float32), -5.5, 5.5)
    return (query_base, key_base)


def draw_queries(key, part):
    return draw_pair(key)[0].astype(jnp.bfloat16)


def draw_key_rows(key, part):
    return draw_pair(key)[1].astype(jnp.bfloat16)


def set_ends(values, own_key, smallest, high):
    spot = [jax.random.randint(jax.random.fold_in(own_key, axis), (), 0, length) for axis, length in enumerate(values.shape)]
    main_axis = values.shape.index(max(values.shape))
    neighbour = spot[:main_axis] + [(spot[main_axis] + 1) % values.shape[main_axis]] + spot[main_axis + 1:]
    return values.at[tuple(spot)].set(smallest).at[tuple(neighbour)].set(high)


def steps_of(rng, shape, shards, least, top_value):
    gain, own = 1.0, jax.random.fold_in(rng, 6)
    for position, blocks in shards:
        draws = jnp.exp(jax.random.uniform(jax.random.fold_in(own, position), (blocks,), jnp.float32, least / len(shards), top_value / len(shards)))
        gain = gain * jnp.repeat(draws, shape[position] // blocks).reshape([-1 if axis == position else 1 for axis in range(len(shape))])
    return gain


def scatter_about(stream_key, shape, spread, reach, cuts=(), held_as=jnp.bfloat16):
    values = jax.random.normal(stream_key, shape, jnp.float32) * spread
    if len(cuts) > 0:
        values = steps_of(stream_key, shape, cuts, -0.22, 0.18) * values
    return jnp.clip(values, min=-reach, max=reach).astype(held_as)


def setup_inputs(seed: int = 0, part: int = 0) -> dict:
    streams_of = jax.random.split(jax.random.key(seed), 10)
    part_keys = jax.random.split(jax.random.fold_in(streams_of[9], part), 10)
    token_ids = set_ends(jax.random.randint(part_keys[0], (LENGTH,), 0, VOCAB), jax.random.fold_in(part_keys[0], 1), 0, VOCAB - 1).astype(jnp.int32)
    embedding = scatter_about(streams_of[1], (VOCAB, D), 0.5, 3.0, (), jnp.float32)
    queries = draw_queries(jax.random.fold_in(jax.random.fold_in(streams_of[9], part), 71), part)
    key_rows = draw_key_rows(jax.random.fold_in(jax.random.fold_in(streams_of[9], part), 71), part)
    value_rows = scatter_about(part_keys[4], (LENGTH, QKV), 1.0, 6.0, ((0, 8),))
    head_mixer = scatter_about(streams_of[5], (QKV, D), QKV ** -0.5, 0.21875)
    expand_weight = scatter_about(streams_of[6], (D, FF), D ** -0.5, 0.15625, ((1, 4),))
    reduce_weight = scatter_about(streams_of[7], (FF, D), FF ** -0.5, 0.109375, ((0, 4),))
    cotangent = scatter_about(part_keys[8], (LENGTH, D), 0.05, 0.29882812, ((0, 8),))
    return {"token_ids": token_ids, "embedding": embedding, "queries": queries, "key_rows": key_rows, "value_rows": value_rows, "head_mixer": head_mixer, "expand_weight": expand_weight, "reduce_weight": reduce_weight, "cotangent": cotangent}


def reference(token_ids, embedding, queries, key_rows, value_rows, head_mixer, expand_weight, reduce_weight, cotangent):
    length = token_ids.shape[0]
    onehot = (token_ids[:, None] == jnp.arange(VOCAB, dtype=jnp.int32)[None, :]).astype(jnp.float32)
    embedded = jnp.dot(onehot, embedding, precision=lax.Precision.HIGHEST, preferred_element_type=jnp.float32)
    block_rows = 512 if length % 512 == 0 else length
    key_heads = key_rows.astype(jnp.float32).reshape(length, FINE_HEADS, HEAD)
    value_heads = value_rows.astype(jnp.float32).reshape(length, FINE_HEADS, HEAD)
    positions = jnp.arange(length, dtype=jnp.int32)

    def attend(packed):
        query_block, first_row = packed
        query_heads = query_block.astype(jnp.float32).reshape(block_rows, FINE_HEADS, HEAD)
        scores = jnp.einsum('rhd,khd->hrk', query_heads, key_heads) * HEAD ** (-0.5)
        query_position = first_row + jnp.arange(block_rows, dtype=jnp.int32)
        allowed = (positions[None, :] <= query_position[:, None])[None]
        scores = jnp.where(allowed, scores, -1e+30)
        row_max = scores.max(-1, keepdims=True)
        weights = jnp.where(allowed, jnp.exp(scores - row_max), 0.0)
        totals = weights.sum(-1)
        summed = jnp.einsum('hrk,khd->hrd', weights.astype(jnp.bfloat16).astype(jnp.float32), value_heads)
        result = summed / totals[..., None]
        return result.transpose(1, 0, 2).reshape(block_rows, QKV).astype(jnp.bfloat16)
    starts = jnp.arange(0, length, block_rows, dtype=jnp.int32)
    attended = lax.map(attend, (queries.reshape(-1, block_rows, QKV), starts)).reshape(length, QKV)
    stream = embedded + jnp.dot(attended, head_mixer, preferred_element_type=jnp.float32)
    shifted = jnp.concatenate([jnp.zeros((1, D), jnp.float32), stream[:-1]], 0)
    pooled = shifted.reshape(-1, POOL, D).mean(axis=1).astype(jnp.bfloat16)
    pooled_float = pooled.astype(jnp.float32)
    normed = (pooled_float * lax.rsqrt(lax.optimization_barrier(jnp.mean(pooled_float * pooled_float, -1, keepdims=True)) + 1e-06)).astype(jnp.bfloat16)
    expanded = jnp.dot(normed, expand_weight, preferred_element_type=jnp.float32)
    activated = jax.nn.gelu(expanded).astype(jnp.bfloat16)
    middle = pooled_float + jnp.dot(activated, reduce_weight, preferred_element_type=jnp.float32)
    before = jnp.concatenate([jnp.zeros((1, D), jnp.float32), middle[:-1]], 0)
    steps_index = jnp.arange(POOL, dtype=jnp.float32)
    after_weights = (steps_index + 1.0) / POOL
    before_weights = (POOL - 1.0 - steps_index) / POOL
    upsampled = (middle[:, None, :] * after_weights[None, :, None] + before[:, None, :] * before_weights[None, :, None]).reshape(length, D)
    restored = (stream + upsampled).astype(jnp.bfloat16)
    grad_rows = cotangent.astype(jnp.float32).reshape(-1, POOL, D)
    own_part = jnp.einsum('sid,i->sd', grad_rows, after_weights)
    later_part = jnp.einsum('sid,i->sd', grad_rows, before_weights)
    middle_grad = (own_part + jnp.concatenate([later_part[1:], jnp.zeros((1, D), jnp.float32)], 0)).astype(jnp.bfloat16)
    act_grad = jnp.dot(middle_grad, reduce_weight.T, preferred_element_type=jnp.float32)
    pre_grad = jax.vjp(jax.nn.gelu, expanded)[1](act_grad)[0].astype(jnp.bfloat16)
    expand_grad = jnp.dot(normed.T, pre_grad, preferred_element_type=jnp.float32)
    reduce_grad = jnp.dot(activated.T, middle_grad, preferred_element_type=jnp.float32)
    return (restored, expand_grad, reduce_grad)
```

```python
import functools

import jax
import jax.numpy as jnp
from jax import lax
from jax.experimental import pallas as pl
from jax.experimental.pallas import tpu as pltpu
from jax.sharding import PartitionSpec as P

FINE_HEADS = 6
HEAD = 128
VOCAB = 6
POOL = 8


NEGATIVE = -1e30


def from_behind(array, axis, by):
    size = lax.axis_size(axis)
    pairs = [(i, i + by) for i in range(size) if 0 <= i + by < size]
    return lax.ppermute(array, axis, pairs)


def empty_state(query_count):
    return (
        jnp.full((FINE_HEADS, query_count), NEGATIVE, jnp.float32),
        jnp.zeros((FINE_HEADS, query_count), jnp.float32),
        jnp.zeros((FINE_HEADS, query_count, HEAD), jnp.float32),
    )


def attend(fold_state, query_block, query_position, key_block, value_block, key_position):
    maxima, totals, summed = fold_state
    query_count = query_block.shape[0]
    key_count = key_block.shape[0]
    query_heads = query_block.reshape(query_count, FINE_HEADS, HEAD)
    key_heads = key_block.reshape(key_count, FINE_HEADS, HEAD)
    value_heads = value_block.reshape(key_count, FINE_HEADS, HEAD)
    scores = jnp.einsum(
        "rhd,khd->hrk", query_heads, key_heads, preferred_element_type=jnp.float32
    ) * HEAD ** (-0.5)
    allowed = (key_position[None, :] <= query_position[:, None])[None]
    scores = jnp.where(allowed, scores, NEGATIVE)
    highest = jnp.maximum(maxima, scores.max(-1))
    weights = jnp.where(allowed, jnp.exp(scores - highest[..., None]), 0.0)
    factor = jnp.exp(maxima - highest)
    totals = totals * factor + weights.sum(-1)
    summed = summed * factor[..., None] + jnp.einsum(
        "hrk,khd->hrd",
        weights.astype(jnp.bfloat16),
        value_heads,
        preferred_element_type=jnp.float32,
    )
    return (highest, totals, summed)


def finish(fold_state):
    maxima, totals, summed = fold_state
    result = summed / totals[..., None]
    return result.transpose(1, 0, 2).reshape(summed.shape[1], -1).astype(jnp.bfloat16)


def key_block_rows():
    return 512


def local(
    token_ids,
    embedding,
    queries,
    key_rows,
    value_rows,
    head_mixer,
    expand_weight,
    reduce_weight,
    cotangent,
):
    shard_rows = queries.shape[0]
    self_index = lax.axis_index(("blk", "wide"))
    query_position = self_index * shard_rows + jnp.arange(shard_rows, dtype=jnp.int32)
    last_position = self_index * shard_rows + shard_rows - 1
    key_piece = lax.all_gather(key_rows, ("blk", "wide"), axis=0, tiled=True)
    value_piece = lax.all_gather(value_rows, ("blk", "wide"), axis=0, tiled=True)
    block_rows = key_block_rows()

    def step(block_index, carry_state):
        offset = block_index * block_rows
        key_block = lax.dynamic_slice_in_dim(key_piece, offset, block_rows, 0)
        value_block = lax.dynamic_slice_in_dim(value_piece, offset, block_rows, 0)
        key_position = offset + jnp.arange(block_rows, dtype=jnp.int32)
        return lax.cond(
            offset <= last_position,
            lambda current: attend(
                current, queries, query_position, key_block, value_block, key_position
            ),
            lambda current: current,
            carry_state,
        )

    attended = finish(
        lax.fori_loop(0, key_piece.shape[0] // block_rows, step, empty_state(shard_rows))
    )
    onehot = (token_ids[:, None] == jnp.arange(VOCAB, dtype=jnp.int32)[None, :]).astype(jnp.float32)
    stream = jnp.dot(
        onehot, embedding, precision=lax.Precision.HIGHEST, preferred_element_type=jnp.float32
    )
    stream = stream + jnp.dot(attended, head_mixer, preferred_element_type=jnp.float32)
    carried = from_behind(stream[-1:], ("blk", "wide"), 1)
    shifted = jnp.concatenate([carried, stream[:-1]], 0)
    pooled = shifted.reshape(-1, POOL, stream.shape[1]).mean(axis=1).astype(jnp.bfloat16)
    pooled_wide = lax.all_gather(pooled, "wide", axis=0, tiled=True)
    pooled_float = pooled_wide.astype(jnp.float32)
    normed = (
        pooled_float * lax.rsqrt(jnp.mean(pooled_float * pooled_float, -1, keepdims=True) + 1e-06)
    ).astype(jnp.bfloat16)
    expanded = jnp.dot(normed, expand_weight, preferred_element_type=jnp.float32)
    activated = jax.nn.gelu(expanded).astype(jnp.bfloat16)
    middle = pooled.astype(jnp.float32) + lax.psum_scatter(
        jnp.dot(activated, reduce_weight, preferred_element_type=jnp.float32).astype(jnp.bfloat16),
        "wide",
        scatter_dimension=0,
        tiled=True,
    ).astype(jnp.float32)
    earlier = from_behind(middle[-1:], ("blk", "wide"), 1)
    before = jnp.concatenate([earlier, middle[:-1]], 0)
    steps_index = jnp.arange(POOL, dtype=jnp.float32)
    after_weights = (steps_index + 1.0) / POOL
    before_weights = (POOL - 1.0 - steps_index) / POOL
    upsampled = (
        middle[:, None, :] * after_weights[None, :, None]
        + before[:, None, :] * before_weights[None, :, None]
    ).reshape(stream.shape)
    restored = (stream + upsampled).astype(jnp.bfloat16)
    grad_rows = cotangent.astype(jnp.float32).reshape(-1, POOL, stream.shape[1])
    own_part = jnp.einsum("sid,i->sd", grad_rows, after_weights)
    later_part = jnp.einsum("sid,i->sd", grad_rows, before_weights)
    following = from_behind(later_part[:1], ("blk", "wide"), -1)
    middle_grad = (own_part + jnp.concatenate([later_part[1:], following], 0)).astype(jnp.bfloat16)
    grad_wide = lax.all_gather(middle_grad, "wide", axis=0, tiled=True)
    act_grad = lax.dot_general(
        grad_wide, reduce_weight, (((1,), (1,)), ((), ())), preferred_element_type=jnp.float32
    )
    pre_grad = jax.vjp(jax.nn.gelu, expanded)[1](act_grad)[0].astype(jnp.bfloat16)
    normed_cols, grad_cols = (
        lax.all_to_all(normed, "blk", split_axis=1, concat_axis=0, tiled=True),
        lax.all_to_all(grad_wide, "blk", split_axis=1, concat_axis=0, tiled=True),
    )
    pre_all, act_all = (
        lax.all_gather(pre_grad, "blk", axis=0, tiled=True),
        lax.all_gather(activated, "blk", axis=0, tiled=True),
    )
    expand_grad = jnp.einsum("gi,gj->ij", normed_cols, pre_all, preferred_element_type=jnp.float32)
    reduce_grad = jnp.einsum("gi,gj->ij", act_all, grad_cols, preferred_element_type=jnp.float32)
    return (restored, expand_grad, reduce_grad)


MIXED = jnp.bfloat16
WIDE_AXES = ("blk", "wide")


def swap(array, axis, distance):
    size = lax.axis_size(axis)
    return lax.ppermute(array, axis, [(i, i ^ distance) for i in range(size)])


def place():
    return lax.axis_index("blk") * lax.axis_size("wide") + lax.axis_index("wide")


def call(kernel, outputs, scratch, *operands):
    spec = pl.BlockSpec(memory_space=pltpu.VMEM)
    return pl.pallas_call(
        kernel,
        out_shape=outputs,
        in_specs=[spec] * len(operands),
        out_specs=jax.tree.map(lambda _: spec, outputs),
        scratch_shapes=scratch,
    )(*operands)


def head_slot(devices):
    return (devices - FINE_HEADS) // 2


def lanes(start, size):
    return pl.ds(pl.multiple_of(start, 128), size)


def rows_at(start, size, step):
    return pl.ds(pl.multiple_of(start, step), size)


def pack_kernel(devices, q_ref, k_ref, v_ref, *piece_refs):
    me = place()
    for distance in range(devices):
        head = jnp.clip((me ^ distance) - head_slot(devices), 0, FINE_HEADS - 1)
        columns = lanes(head * HEAD, HEAD)
        for part, source in enumerate((q_ref, k_ref, v_ref)):
            piece_refs[distance][:, part * HEAD:(part + 1) * HEAD] = source[:, columns]


def grad_kernel(cot_ref, token_ref, out_ref, row_ref):
    shard_rows, width = cot_ref.shape
    short = shard_rows // POOL
    j = lax.broadcasted_iota(jnp.int32, (short + POOL, shard_rows), 0)
    t = lax.broadcasted_iota(jnp.int32, (short + POOL, shard_rows), 1)
    group, i = t // POOL, (t % POOL).astype(jnp.float32)
    after = (i + 1.0) / POOL
    before = (POOL - 1.0 - i) / POOL
    own = jnp.where(group == j, after, jnp.where(group == j + 1, before, 0.0))
    first = jnp.where(group == 0, before, 0.0)
    combine = jnp.where(j < short, own, first).astype(MIXED)
    grads = jnp.dot(combine, cot_ref[...], preferred_element_type=jnp.float32)
    out_ref[:, :width] = grads[:short].astype(MIXED)
    row_ref[...] = jnp.zeros_like(row_ref)
    for k in range(width // 128):
        row_ref[k:k + 1, :] = grads[short:short + 1, k * 128:(k + 1) * 128]
    out_ref[:, width:width + 128] = row_ref[...].astype(MIXED)
    tokens = jnp.broadcast_to(token_ref[...], (short, shard_rows)).astype(jnp.float32)
    spread = jnp.where(group[:short] == j[:short], tokens, 0.0).astype(MIXED)
    r = lax.broadcasted_iota(jnp.int32, (shard_rows, 128), 0)
    c = lax.broadcasted_iota(jnp.int32, (shard_rows, 128), 1)
    fold = jnp.where(r % POOL == c, 1.0, 0.0).astype(MIXED)
    out_ref[:, width + 128:] = jnp.dot(spread, fold, preferred_element_type=jnp.float32).astype(MIXED)


def attention_kernel(devices, *refs):
    pieces, outs = refs[:devices], refs[devices:2 * devices]
    q_s, k_s, v_s, att_s = refs[2 * devices:]
    shard_rows = pieces[0].shape[0]
    total = shard_rows * devices
    short = total // POOL
    me = place()
    head = me - head_slot(devices)
    owner = jnp.logical_and(head >= 0, head < FINE_HEADS)

    @pl.when(owner)
    def _():
        for distance in range(devices):
            rows = rows_at((me ^ distance) * shard_rows, shard_rows, shard_rows)
            for part, target in enumerate((q_s, k_s, v_s)):
                target[rows, :] = pieces[distance][:, part * HEAD:(part + 1) * HEAD]
        block = 2 * shard_rows
        for first in range(0, total, block):
            keys = first + block
            scores = lax.dot_general(
                q_s[first:keys, :], k_s[:keys, :], (((1,), (1,)), ((), ())),
                preferred_element_type=jnp.float32,
            )
            r = lax.broadcasted_iota(jnp.int32, (block, block), 0)
            c = lax.broadcasted_iota(jnp.int32, (block, block), 1)
            diagonal = jnp.where(c <= r, scores[:, first:], NEGATIVE)
            highest = diagonal.max(-1, keepdims=True)
            if first:
                highest = jnp.maximum(highest, scores[:, :first].max(-1, keepdims=True))
            scale = HEAD ** (-0.5)
            weights = jnp.exp((diagonal - highest) * scale)
            totals = weights.sum(-1, keepdims=True)
            summed = jnp.dot(weights.astype(MIXED), v_s[first:keys, :], preferred_element_type=jnp.float32)
            if first:
                weights = jnp.exp((scores[:, :first] - highest) * scale)
                totals = totals + weights.sum(-1, keepdims=True)
                summed = summed + jnp.dot(weights.astype(MIXED), v_s[:first, :], preferred_element_type=jnp.float32)
            att_s[first:keys, :] = (summed / totals).astype(MIXED)
        j = lax.broadcasted_iota(jnp.int32, (short, total), 0)
        t = lax.broadcasted_iota(jnp.int32, (short, total), 1)
        inside = jnp.logical_and(t >= POOL * j - 1, t < POOL * j + POOL - 1)
        pooled = jnp.dot(
            jnp.where(inside, 1.0 / POOL, 0.0).astype(MIXED), att_s[...], preferred_element_type=jnp.float32
        ).astype(MIXED)
        for distance in range(devices):
            outs[distance][:short, :] = pooled
            rows = rows_at((me ^ distance) * shard_rows, shard_rows, shard_rows)
            outs[distance][short:, :] = att_s[rows, :]

    @pl.when(jnp.logical_not(owner))
    def _():
        for out in outs:
            out[...] = jnp.zeros_like(out)


def split_dot(exact, table):
    high = table.astype(MIXED)
    low = (table - high.astype(jnp.float32)).astype(MIXED)
    return jnp.dot(exact, high, preferred_element_type=jnp.float32) + jnp.dot(
        exact, low, preferred_element_type=jnp.float32
    )


GELU_A = 0.7978845608028654
GELU_B = 0.044715


def gelu_tanh(x):
    return jnp.tanh(GELU_A * (x + GELU_B * x * x * x))


def middle_kernel(devices, wide, blk, *refs):
    pieces = refs[:devices]
    grads = refs[devices:devices + blk]
    mixer_ref, table_ref, up_ref, down_ref = refs[devices + blk:devices + blk + 4]
    outs = refs[devices + blk + 4:]
    parts = outs[:wide]
    pooled_ref, normed_ref, expanded_ref, activated_ref, att_ref = outs[wide:wide + 5]
    pa_s, tok_s, pool_s, part_s, row_s = outs[wide + 5:]
    total_short = pa_s.shape[0]
    short = total_short // devices
    width = mixer_ref.shape[1]
    me = place()
    b, z = lax.axis_index("blk"), lax.axis_index("wide")
    for distance in range(devices):
        head = (me ^ distance) - head_slot(devices)

        @pl.when(jnp.logical_and(head >= 0, head < FINE_HEADS))
        def _():
            columns = lanes(head * HEAD, HEAD)
            pa_s[:, columns] = pieces[distance][:total_short, :]
            att_ref[:, columns] = pieces[distance][total_short:, :]

    for across in range(blk):
        for along in range(wide):
            source = (b ^ across) * wide + (z ^ along)
            tok_s[rows_at(POOL + source * short, short, POOL), :] = grads[across][along, :, width + 128:].astype(jnp.float32)
    tok_s[:POOL, :] = jnp.full((POOL, 128), -1.0, jnp.float32)
    tokens = tok_s[POOL:, :]
    earlier = tok_s[POOL - 1:POOL - 1 + total_short, :]
    lane = lax.broadcasted_iota(jnp.int32, (total_short, 128), 1)
    counts = jnp.zeros((total_short, 128), jnp.float32)
    for token in range(VOCAB):
        hits = jnp.where(jnp.logical_and(lane < POOL - 1, tokens == token), 1.0, 0.0)
        hits = hits + jnp.where(jnp.logical_and(lane == POOL - 1, earlier == token), 1.0, 0.0)
        counts = counts + jnp.where(lane == token, hits.sum(-1, keepdims=True), 0.0)
    counts = (counts * (1.0 / POOL)).astype(MIXED)[:, :POOL]
    pooled = jnp.dot(pa_s[...], mixer_ref[...], preferred_element_type=jnp.float32)
    pooled = (pooled + split_dot(counts, table_ref[...])).astype(MIXED)
    pooled_float = pooled.astype(jnp.float32)
    pool_s[:POOL, :] = jnp.zeros((POOL, width), jnp.float32)
    pool_s[POOL:, :] = pooled_float
    square = jnp.mean(pooled_float * pooled_float, -1, keepdims=True)
    normed = (pooled_float * lax.rsqrt(square + 1e-06)).astype(MIXED)
    normed_ref[...] = normed
    expanded = jnp.dot(normed, up_ref[...], preferred_element_type=jnp.float32)
    expanded_ref[...] = expanded
    activated = (0.5 * expanded * (1.0 + gelu_tanh(expanded))).astype(MIXED)
    activated_ref[...] = activated
    part_s[:POOL, :] = jnp.zeros((POOL, width), jnp.float32)
    part_s[POOL:, :] = jnp.dot(activated, down_ref[...], preferred_element_type=jnp.float32)
    row_s[...] = jnp.zeros_like(row_s)
    for along in range(wide):
        start = (b * wide + (z ^ along)) * short
        window = part_s[rows_at(start, POOL + short, POOL), :]
        parts[along][:, :width] = window[POOL:].astype(MIXED)
        for k in range(width // 128):
            row_s[k:k + 1, :] = window[POOL - 1:POOL, k * 128:(k + 1) * 128]
        parts[along][:, width:] = row_s[...].astype(MIXED)
    pooled_ref[...] = pool_s[rows_at(me * short, POOL + short, POOL), :]


def weights_kernel(devices, wide, blk, *refs):
    grads = refs[:blk]
    down_ref, expanded_ref, normed_ref, activated_ref = refs[blk:blk + 4]
    up_grad_ref, down_grad_ref, grad_s, late_s, mixed_s = refs[blk + 4:]
    width = down_ref.shape[1]
    short = grads[0].shape[1]
    b, z = lax.axis_index("blk"), lax.axis_index("wide")
    for across in range(blk):
        for along in range(wide):
            source = (b ^ across) * wide + (z ^ along)
            piece = grads[across]
            grad_s[rows_at(source * short, short, POOL), :] = piece[along, :, :width].astype(jnp.float32)
            row = piece[along, :, width:width + 128].astype(jnp.float32)
            for k in range(width // 128):
                late_s[rows_at(source * POOL, 1, POOL), k * 128:(k + 1) * 128] = row[k:k + 1, :]
    for source in range(devices - 1):
        last = source * short + short - 1
        grad_s[last:last + 1, :] += late_s[(source + 1) * POOL:(source + 1) * POOL + 1, :]
    mixed_s[...] = grad_s[...].astype(MIXED)
    act_grad = lax.dot_general(
        mixed_s[...], down_ref[...], (((1,), (1,)), ((), ())), preferred_element_type=jnp.float32
    )
    x = expanded_ref[...]
    t = gelu_tanh(x)
    slope = 0.5 * (1.0 + t) + 0.5 * x * (1.0 - t * t) * (GELU_A * (1.0 + 3.0 * GELU_B * x * x))
    pre_grad = (act_grad * slope).astype(MIXED)
    share = up_grad_ref.shape[0]
    columns = lanes(b * share, share)
    contract = (((0,), (0,)), ((), ()))
    up_grad_ref[...] = lax.dot_general(normed_ref[:, columns], pre_grad, contract, preferred_element_type=jnp.float32)
    down_grad_ref[...] = lax.dot_general(activated_ref[...], mixed_s[:, columns], contract, preferred_element_type=jnp.float32)


def stream_kernel(att_ref, mixer_ref, table_ref, token_ref, out_ref):
    shard_rows = att_ref.shape[0]
    which = lax.broadcasted_iota(jnp.int32, (table_ref.shape[0], shard_rows), 0)
    onehot = jnp.where(which == token_ref[...], 1.0, 0.0).astype(jnp.float32).T.astype(MIXED)
    out_ref[...] = split_dot(onehot, table_ref[...]) + jnp.dot(
        att_ref[...], mixer_ref[...], preferred_element_type=jnp.float32
    )


def final_kernel(wide, *refs):
    parts = refs[:wide]
    pooled_ref, stream_ref, out_ref, mid_s = refs[wide:]
    short = parts[0].shape[0]
    width = stream_ref.shape[1]
    summed = sum(part[...].astype(jnp.float32) for part in parts)
    mid_s[...] = pooled_ref[...]
    mid_s[POOL:, :] += summed[:, :width]
    inside = jnp.where(place() > 0, 1.0, 0.0)
    for k in range(width // 128):
        columns = slice(k * 128, (k + 1) * 128)
        mid_s[POOL - 1:POOL, columns] = (mid_s[POOL - 1:POOL, columns] + summed[k:k + 1, width:]) * inside
    i = lax.broadcasted_iota(jnp.int32, (POOL, 128), 0).astype(jnp.float32)[:, :1]
    after = (i + 1.0) / POOL
    before = (POOL - 1.0 - i) / POOL
    for pair in range(short // 2):
        halves = []
        for j in (2 * pair, 2 * pair + 1):
            now = mid_s[POOL + j:POOL + j + 1, :]
            prior = mid_s[POOL + j - 1:POOL + j, :]
            halves.append(stream_ref[j * POOL:(j + 1) * POOL, :] + (now * after + prior * before))
        out_ref[pair * 2 * POOL:(pair + 1) * 2 * POOL, :] = jnp.concatenate(halves, 0).astype(MIXED)


def by_head(
    token_ids,
    embedding,
    queries,
    key_rows,
    value_rows,
    head_mixer,
    expand_weight,
    reduce_weight,
    cotangent,
):
    blk, wide = lax.axis_size("blk"), lax.axis_size("wide")
    devices = blk * wide
    shard_rows, qkv = queries.shape
    width = head_mixer.shape[1]
    hidden = expand_weight.shape[1]
    short = shard_rows // POOL
    total_short = devices * short
    total = devices * shard_rows
    shape = jax.ShapeDtypeStruct
    float32 = jnp.float32
    pieces = call(
        functools.partial(pack_kernel, devices),
        [shape((shard_rows, 3 * HEAD), MIXED)] * devices,
        [],
        queries, key_rows, value_rows,
    )
    pieces = [pieces[0]] + [swap(pieces[d], WIDE_AXES, d) for d in range(1, devices)]
    tokens = token_ids.reshape(1, shard_rows)
    table = jnp.pad(embedding, ((0, POOL - VOCAB), (0, 0)))
    grad_piece = call(
        grad_kernel, shape((short, width + 256), MIXED), [pltpu.VMEM((short, 128), float32)], cotangent, tokens
    )
    stack = jnp.stack([grad_piece] + [swap(grad_piece, "wide", d) for d in range(1, wide)])
    stacks = [stack] + [swap(stack, "blk", d) for d in range(1, blk)]
    outs = call(
        functools.partial(attention_kernel, devices),
        [shape((total_short + shard_rows, HEAD), MIXED)] * devices,
        [pltpu.VMEM((total, HEAD), MIXED)] * 4,
        *pieces,
    )
    outs = [outs[0]] + [swap(outs[d], WIDE_AXES, d) for d in range(1, devices)]
    results = call(
        functools.partial(middle_kernel, devices, wide, blk),
        [shape((short, width + 128), MIXED)] * wide
        + [
            shape((POOL + short, width), float32),
            shape((total_short, width), MIXED),
            shape((total_short, hidden), float32),
            shape((total_short, hidden), MIXED),
            shape((shard_rows, qkv), MIXED),
        ],
        [
            pltpu.VMEM((total_short, qkv), MIXED),
            pltpu.VMEM((POOL + total_short, 128), float32),
            pltpu.VMEM((POOL + total_short, width), float32),
            pltpu.VMEM((POOL + total_short, width), float32),
            pltpu.VMEM((short, 128), float32),
        ],
        *outs, *stacks, head_mixer, table, expand_weight, reduce_weight,
    )
    parts = results[:wide]
    pooled, normed, expanded, activated, attended = results[wide:]
    parts = [parts[0]] + [swap(parts[d], "wide", d) for d in range(1, wide)]
    up_grad, down_grad = call(
        functools.partial(weights_kernel, devices, wide, blk),
        [shape((width // blk, hidden), float32), shape((hidden, width // blk), float32)],
        [
            pltpu.VMEM((total_short, width), float32),
            pltpu.VMEM((devices * POOL, width), float32),
            pltpu.VMEM((total_short, width), MIXED),
        ],
        *stacks, reduce_weight, expanded, normed, activated,
    )
    stream = call(stream_kernel, shape((shard_rows, width), float32), [], attended, head_mixer, table, tokens)
    restored = call(
        functools.partial(final_kernel, wide),
        shape((shard_rows, width), MIXED),
        [pltpu.VMEM((POOL + short, width), float32)],
        *parts, pooled, stream,
    )
    return (restored, up_grad, down_grad)


def fits_by_head(blk, wide):
    devices = blk * wide
    return devices & (devices - 1) == 0 and FINE_HEADS <= devices <= 2 * FINE_HEADS


def solution(mesh):
    blk, wide = mesh.shape["blk"], mesh.shape["wide"]
    return jax.shard_map(
        by_head if fits_by_head(blk, wide) else local,
        mesh=mesh,
        in_specs=(
            P(("dp", "blk", "wide")),
            P(),
            P(("dp", "blk", "wide"), None),
            P(("dp", "blk", "wide"), None),
            P(("dp", "blk", "wide"), None),
            P(),
            P(None, "wide"),
            P("wide", None),
            P(("dp", "blk", "wide"), None),
        ),
        out_specs=(
            P(("dp", "blk", "wide"), None),
            P(("dp", "blk"), "wide"),
            P(("dp", "wide"), "blk"),
        ),
        check_vma=False,
    )
```
